256 devices in a mesh: seq: 32 (over x_lo, z, core), fsdp: 8 (over x_hi, y).
Axes of the slice: x: 4 (x_hi: 2, x_lo: 2; x = x_hi * 2 + x_lo), y: 4, z: 8, core: 2. Of those that a mesh axis runs over, the one named last changes fastest.
Arguments:
- frames_in: bfloat16 [196608, 1536], P(('seq', 'fsdp')), may hold values from -40 to 40
- norm_gain: float32 [1536], replicated, may hold values from 0.1 to 1.9
- in_weight: float32 [1536, 2, 1536], P(None, None, 'fsdp'), may hold values from -0.15625 to 0.15625
- depth_kernel: float32 [31, 1536], replicated, may hold values from -1 to 1
- mid_gain: float32 [1536], replicated, may hold values from 0.1 to 1.9
- mid_bias: float32 [1536], replicated, may hold values from -3 to 3
- out_weight: float32 [1536, 1536], P('fsdp'), may hold values from -0.15625 to 0.15625
Outputs:
- frames_out: bfloat16 [196608, 1536], P(('seq', 'fsdp'))
The draws below stay inside these ranges and needn't reach their ends.
All inputs are finite; a program needn't handle non-finite values.
Results may differ from the reference program's by a relative error of at most 0.005.
Values may be sent and summed in bfloat16 or wider, within the bound.
No kernel may reach another device: no remote copies, remote signals or barrier semaphores. Data moves between devices by JAX's collectives and lax.ppermute only.
A program may use at most 64 MiB of HBM per device.

```python
import math
import jax
import jax.numpy as jnp
from jax import lax

D = 1536
KERNEL = 31
TOK_DEV = 768
FRAMES = 196608


def draw_frames_in(key, part):
    key_rows = jax.random.fold_in(key, 11)
    key_cols = jax.random.fold_in(key, 23)
    key_noise = jax.random.fold_in(key, 37)
    row_scale = jnp.exp(jax.random.uniform(key_rows, (FRAMES, 1), jnp.float32, math.log(0.3), math.log(3.0)))
    col_scale = jnp.exp(jax.random.uniform(key_cols, (1, D), jnp.float32, math.log(0.3), math.log(3.0)))
    noise_part = jax.random.truncated_normal(key_noise, -4.0, 4.0, (FRAMES, D), jnp.float32)
    values = noise_part * row_scale * col_scale
    return values.astype(jnp.bfloat16)


def steps_of(rng, extent, split, low, top_value):
    def one(axis_at, parts):
        draws = jax.random.uniform(jax.random.fold_in(jax.random.fold_in(rng, 6), axis_at), (parts,), jnp.float32, low / len(split), top_value / len(split))
        return jnp.repeat(jnp.exp(draws), extent[axis_at] // parts).reshape((-1,) + (1,) * (len(extent) - axis_at - 1))

    loudness = one(*split[0])
    for cut in split[1:]:
        loudness = loudness * one(*cut)
    return loudness


def noise(key, shape, scale, bound, pieces=(), held_as=jnp.bfloat16):
    values = scale * jax.random.normal(key, shape, jnp.float32)
    if pieces:
        values = values * steps_of(key, shape, pieces, -0.22, 0.18)
    return jnp.clip(values, -bound, bound).astype(held_as)


def setup_inputs(seed: int = 0) -> dict:
    arg_keys = jax.random.split(jax.random.key(seed), 8)
    return {
        "frames_in": draw_frames_in(jax.random.fold_in(arg_keys[7], 71), 0),
        "norm_gain": jnp.clip(1.0 + 0.18 * jax.random.normal(arg_keys[1], (D,), jnp.float32), 0.1, 1.9),
        "in_weight": noise(arg_keys[2], (D, 2, D), D ** -0.5, 0.15625, ((2, 8),), jnp.float32),
        "depth_kernel": noise(arg_keys[3], (KERNEL, D), KERNEL ** -0.5, 1.0, (), jnp.float32),
        "mid_gain": jnp.clip(1.0 + 0.18 * jax.random.normal(arg_keys[4], (D,), jnp.float32), 0.1, 1.9),
        "mid_bias": noise(arg_keys[5], (D,), 0.5, 3.0, (), jnp.float32),
        "out_weight": noise(arg_keys[6], (D, D), D ** -0.5, 0.15625, ((0, 8),), jnp.float32),
    }


EPSILON = 1e-05

def layer_norm(values, gain):
    row_mean = lax.optimization_barrier(jnp.mean(values, axis=-1, keepdims=True))
    centred = values - row_mean
    row_var = lax.optimization_barrier(jnp.mean(centred * centred, axis=-1, keepdims=True))
    return centred * lax.rsqrt(row_var + EPSILON) * gain

def depthwise(window, kernel, row_count):
    widened = window.astype(jnp.float32)
    summed = jnp.zeros((row_count, widened.shape[1]), jnp.float32)
    for tap_index in range(kernel.shape[0]):
        summed = summed + kernel[tap_index] * widened[tap_index:tap_index + row_count]
    return summed

def mid_activation(conv, summed, squares, width, gain, bias):
    row_mean = summed / width
    row_var = squares / width - row_mean * row_mean
    middle = (conv - row_mean[:, None]) * lax.rsqrt(row_var + EPSILON)[:, None] * gain + bias
    return (middle * jax.nn.sigmoid(middle)).astype(jnp.bfloat16)

def reference(frames_in, norm_gain, in_weight, depth_kernel, mid_gain, mid_bias, out_weight):
    block_count = FRAMES // TOK_DEV
    halo_rows = KERNEL - 1
    w_in = in_weight.astype(jnp.bfloat16).reshape(D, 2 * D)
    w_out = out_weight.astype(jnp.bfloat16)

    def block_step(prior_rows, block):
        values = block.astype(jnp.float32)
        normed = layer_norm(values, norm_gain).astype(jnp.bfloat16)
        projected = jnp.dot(normed, w_in, preferred_element_type=jnp.float32)
        gated = (projected[:, :D] * jax.nn.sigmoid(projected[:, D:])).astype(jnp.bfloat16)
        window = jnp.concatenate([prior_rows, gated], axis=0)
        conv = depthwise(window, depth_kernel, TOK_DEV)
        activ = mid_activation(conv, lax.optimization_barrier(jnp.sum(conv, axis=1)), lax.optimization_barrier(jnp.sum(conv * conv, axis=1)), D, mid_gain, mid_bias)
        result = (values + jnp.dot(activ, w_out, preferred_element_type=jnp.float32)).astype(jnp.bfloat16)
        return (gated[TOK_DEV - halo_rows:], result)
    start_rows = jnp.zeros((halo_rows, D), jnp.bfloat16)
    _, outputs = lax.scan(block_step, start_rows, frames_in.reshape(block_count, TOK_DEV, D))
    return outputs.reshape(FRAMES, D)
```

```python
import jax
import jax.numpy as jnp
from jax import lax
from jax.experimental import pallas as pl
from jax.experimental.pallas import tpu as pltpu
from jax.sharding import PartitionSpec as P

EPSILON = 1e-05
AXES = ("seq", "fsdp")
HALO = 32
LANES = 128


def place(x, y, z, core):
    x, y, z, core = x % 4, y % 4, z % 8, core % 2
    return (((x % 2) * 8 + z) * 2 + core) * 8 + (x // 2) * 4 + y


def route(target):
    return [
        (place(x, y, z, c), place(*target(x, y, z, c)))
        for x in range(4)
        for y in range(4)
        for z in range(8)
        for c in range(2)
    ]


OUTWARD = route(lambda x, y, z, c: (x, y - 1 if c == 0 else y + 1, z, c))
BACK = route(lambda x, y, z, c: (x, y + 1 if c == 0 else y - 1, z, c))
CROSS = route(lambda x, y, z, c: (((x + 1) ^ 1) - 1, y, z, c))
SIBLING = route(lambda x, y, z, c: (x, y, z, 1 - c))


def moved(value, pairs):
    return lax.ppermute(value, AXES, pairs)


def norm_kernel(halo_ref, x_ref, gain_ref, out_ref):
    gain = gain_ref[...]

    def normed(values):
        values = values.astype(jnp.float32)
        centred = values - jnp.mean(values, axis=-1, keepdims=True)
        var = jnp.mean(centred * centred, axis=-1, keepdims=True)
        return (centred * lax.rsqrt(var + EPSILON) * gain).astype(jnp.bfloat16)

    out_ref[0:HALO, :] = normed(halo_ref[...])
    rows = x_ref.shape[0]
    step = 64

    @pl.loop(0, rows // step)
    def _(i):
        at = pl.multiple_of(i * step, step)
        out_ref[pl.ds(HALO + at, step), :] = normed(x_ref[pl.ds(at, step), :])


def group_kernel(taps, count, *refs):
    nx_ref, dk_ref = refs[:2]
    pieces = refs[2 : 2 + count]
    conv_ref, s1_ref, s2_ref, w_ref, gated_ref = refs[2 + count :]
    rows = conv_ref.shape[0]
    tiles = conv_ref.shape[1] // LANES
    first = 0
    for piece in pieces:
        size = piece.shape[1]
        done = 0
        while done < size:
            tile, at = divmod(first + done, LANES)
            part = min(size - done, LANES - at)
            for side in range(2):
                w_ref[tile, side * LANES + at : side * LANES + at + part, :] = piece[
                    side, done : done + part, :
                ]
            done += part
        first += size
    s1_ref[...] = jnp.zeros_like(s1_ref)
    s2_ref[...] = jnp.zeros_like(s2_ref)

    def project(tile):
        both = lax.dot_general(
            nx_ref[...], w_ref[tile], (((1,), (1,)), ((), ())), preferred_element_type=jnp.float32
        )
        gated = both[:, :LANES] * jax.nn.sigmoid(both[:, LANES:])
        gated_ref[tile % 2] = gated.astype(jnp.bfloat16).astype(jnp.float32)

    def convolve(tile):
        lanes = slice(tile * LANES, (tile + 1) * LANES)
        step = 32
        source = gated_ref.at[tile % 2]
        for at in range(0, rows, step):
            total = None
            for tap in range(taps):
                begin = HALO - (taps - 1) + tap + at
                term = dk_ref[tap : tap + 1, lanes] * source[begin : begin + step, :]
                total = term if total is None else total + term
            conv_ref[at : at + step, lanes] = total.astype(conv_ref.dtype)
            s1_ref[at : at + step, :] += total
            s2_ref[at : at + step, :] += total * total

    for tile in range(tiles + 1):
        if tile < tiles:
            project(tile)
        if tile > 0:
            convolve(tile - 1)


def mix_kernel(count, *refs):
    x_ref, gain_ref, bias_ref = refs[:3]
    convs, s1s, s2s = refs[3:5], refs[5:7], refs[7:9]
    pieces = refs[9 : 9 + count]
    out_ref, w_ref, act_ref = refs[9 + count :]
    first = 0
    for piece in pieces:
        w_ref[first : first + piece.shape[0], :] = piece[...]
        first += piece.shape[0]
    rows, width = x_ref.shape
    half = width // 2
    step = 128

    @pl.loop(0, rows // step)
    def _(i):
        at = pl.ds(pl.multiple_of(i * step, step), step)
        mean = jnp.sum(s1s[0][at, :] + s1s[1][at, :], axis=1, keepdims=True) / width
        var = jnp.sum(s2s[0][at, :] + s2s[1][at, :], axis=1, keepdims=True) / width - mean * mean
        scale = lax.rsqrt(var + EPSILON)
        for part in range(2):
            lanes = slice(part * half, (part + 1) * half)
            conv = convs[part][at, :].astype(jnp.float32)
            mid = (conv - mean) * scale * gain_ref[:, lanes] + bias_ref[:, lanes]
            act_ref[:, lanes] = (mid * jax.nn.sigmoid(mid)).astype(jnp.bfloat16)
        mixed = jnp.dot(act_ref[...], w_ref[...], preferred_element_type=jnp.float32)
        out_ref[at, :] = (x_ref[at, :].astype(jnp.float32) + mixed).astype(out_ref.dtype)


def params(limit_mib):
    return pltpu.CompilerParams(vmem_limit_bytes=limit_mib * 2**20)


def spread(own):
    size = own.shape[1] // 2
    core = lax.rem(lax.axis_index("seq"), 2)

    def half(value):
        return lax.dynamic_slice_in_dim(value, core * size, size, axis=1)

    beside = moved(own, OUTWARD)
    cross = moved(half(own), CROSS)
    beside_other = moved(beside, SIBLING)
    cross_other = moved(cross, SIBLING)
    far = moved(half(beside), OUTWARD)
    diagonal = moved(cross, OUTWARD)
    diagonal_back = moved(cross, BACK)
    far_other = moved(far, SIBLING)
    opposite = moved(far, CROSS)
    diagonal_other = moved(diagonal, SIBLING)
    diagonal_back_other = moved(diagonal_back, SIBLING)
    opposite_other = moved(opposite, SIBLING)
    return (
        [own, cross, cross_other, beside, beside_other],
        [far, far_other, opposite, opposite_other, diagonal, diagonal_back_other, diagonal_back, diagonal_other],
    )


def channel_blocks():
    core = lax.rem(lax.axis_index("seq"), 2)
    at = lax.axis_index("fsdp")
    high, y = at // 4, lax.rem(at, 4)

    def block(side, dy, part):
        return ((side * 4 + lax.rem(y + dy + 8, 4)) * 2) + part

    toward = 1 - 2 * core
    other = 1 - high
    return jnp.stack(
        [
            block(high, 0, 0), block(high, 0, 1),
            block(other, 0, core), block(other, 0, 1 - core),
            block(high, toward, 0), block(high, toward, 1),
            block(high, -toward, 0), block(high, -toward, 1),
            block(high, 2, core), block(high, 2, 1 - core),
            block(other, 2, core), block(other, 2, 1 - core),
            block(other, toward, core), block(other, toward, 1 - core),
            block(other, -toward, core), block(other, -toward, 1 - core),
        ]
    )


def body(frames_in, norm_gain, in_weight, depth_kernel, mid_gain, mid_bias, out_weight):
    rows, width = frames_in.shape
    taps = depth_kernel.shape[0]
    bf16, f32 = jnp.bfloat16, jnp.float32
    half = width // 2
    order = [(i, i + 1) for i in range(lax.axis_size("seq") * lax.axis_size("fsdp") - 1)]
    halo = moved(frames_in[rows - HALO :], order)
    in_local = jnp.transpose(in_weight.astype(bf16), (1, 2, 0))
    out_local = out_weight.astype(bf16)[None]
    in_near, in_far = spread(in_local)
    out_near, out_far = spread(out_local)

    stacked = jnp.concatenate([depth_kernel, mid_gain[None], mid_bias[None]], axis=0)
    blocks = stacked.reshape(taps + 2, 16, width // 16).transpose(1, 0, 2)
    picked = jnp.take(blocks, channel_blocks(), axis=0).transpose(1, 0, 2).reshape(taps + 2, width)
    kernel, gain, bias = picked[:taps], picked[taps : taps + 1], picked[taps + 1 :]

    normed = pl.pallas_call(
        norm_kernel,
        out_shape=jax.ShapeDtypeStruct((rows + HALO, width), bf16),
        compiler_params=params(16),
        name="norm",
    )(halo, frames_in, norm_gain[None])

    def group(pieces, taps_of):
        flops = 2 * (rows + HALO) * width * width + 2 * taps * rows * half
        return pl.pallas_call(
            lambda *refs: group_kernel(taps, len(pieces), *refs),
            out_shape=(
                jax.ShapeDtypeStruct((rows, half), bf16),
                jax.ShapeDtypeStruct((rows, LANES), f32),
                jax.ShapeDtypeStruct((rows, LANES), f32),
            ),
            scratch_shapes=[
                pltpu.VMEM((half // LANES, 2 * LANES, width), bf16),
                pltpu.VMEM((2, rows + HALO, LANES), f32),
            ],
            compiler_params=params(30),
            cost_estimate=pl.CostEstimate(flops=flops, bytes_accessed=width * width * 2, transcendentals=rows * half),
            name="group",
        )(normed, taps_of, *pieces)

    conv_a, s1_a, s2_a = group(in_near, kernel[:, :half])
    conv_b, s1_b, s2_b = group(in_far, kernel[:, half:])
    pieces = [piece[0] for piece in out_near + out_far]
    return pl.pallas_call(
        lambda *refs: mix_kernel(len(pieces), *refs),
        out_shape=jax.ShapeDtypeStruct((rows, width), bf16),
        scratch_shapes=[pltpu.VMEM((width, width), bf16), pltpu.VMEM((128, width), bf16)],
        compiler_params=params(30),
        cost_estimate=pl.CostEstimate(flops=2 * rows * width * width, bytes_accessed=width * width * 2, transcendentals=rows * width),
        name="mix",
    )(frames_in, gain, bias, conv_a, conv_b, s1_a, s1_b, s2_a, s2_b, *pieces)


def solution(mesh):
    placed = (P(AXES, None), P(), P(None, None, "fsdp"), P(), P(), P(), P("fsdp", None))
    return jax.shard_map(body, mesh=mesh, in_specs=placed, out_specs=P(AXES, None), check_vma=False)
```

```python
import functools

import jax
import jax.numpy as jnp
from jax import lax
from jax.experimental import pallas as pl
from jax.experimental.pallas import tpu as pltpu
from jax.sharding import PartitionSpec as P

EPSILON = 1e-05
AXES = ("seq", "fsdp")
HALO = 32
LANES = 128


def place(x, y, z, core):
    x, y, z, core = x % 4, y % 4, z % 8, core % 2
    return (((x % 2) * 8 + z) * 2 + core) * 8 + (x // 2) * 4 + y


def route(target):
    return [
        (place(x, y, z, c), place(*target(x, y, z, c)))
        for x in range(4)
        for y in range(4)
        for z in range(8)
        for c in range(2)
    ]


def colour(x, z):
    return ((x // 2) ^ x ^ z) & 1


ASIDE = route(lambda x, y, z, c: (x, y - 1 if c == colour(x, z) else y + 1, z, c))
PARTNER = route(lambda x, y, z, c: (x ^ 1, y, z, c) if c == 0 else (x, y, z ^ 1, c))
CROSS = route(lambda x, y, z, c: (((x + 1) ^ 1) - 1, y, z, c))
SIBLING = route(lambda x, y, z, c: (x, y, z, 1 - c))
UNIT = 32


def moved(value, pairs):
    return lax.ppermute(value, AXES, pairs)


def my_core():
    return lax.rem(lax.axis_index("seq"), 2)


def prepare_kernel(w_in, w_out, taps_in, gain_in, bias_in, frames_in, *refs):
    in_mine, in_rest, out_mine, out_rest, picked_ref, halo_ref, in_v, out_v, all_ref, taps_v, gain_v, bias_v, sems = refs
    core = my_core()
    size = in_mine.shape[1]
    taps, width = taps_in.shape
    halves = [pl.ds(pl.multiple_of(which * size, UNIT), size) for which in (core, 1 - core)]
    pairs = [(w_in.at[side, part], in_v.at[side, k]) for side in range(2) for k, part in enumerate(halves)]
    pairs += [(w_out.at[part], out_v.at[k]) for k, part in enumerate(halves)]
    pairs += [
        (taps_in, taps_v),
        (gain_in, gain_v),
        (bias_in, bias_v),
        (frames_in.at[frames_in.shape[0] - HALO :], halo_ref),
    ]
    copies = [pltpu.make_async_copy(source, target, sems.at[i]) for i, (source, target) in enumerate(pairs)]
    for copy in copies:
        copy.start()
    for side in range(2):
        for k, out_ref in enumerate((in_mine, in_rest)):
            copies[2 * side + k].wait()
            out_ref[side] = (0.5 * in_v[side, k]).astype(jnp.bfloat16)
    for k, out_ref in enumerate((out_mine, out_rest)):
        copies[4 + k].wait()
        out_ref[0] = out_v[k].astype(jnp.bfloat16)
    for copy in copies[6:]:
        copy.wait()
    all_ref[0:taps, :] = taps_v[...]
    all_ref[32:33, :] = 0.5 * gain_v[...].reshape(1, width)
    all_ref[33:34, :] = 0.5 * bias_v[...].reshape(1, width)
    at = lax.axis_index("fsdp")
    high, y = at // 4, lax.rem(at, 4)
    half, shard = width // 2, width // 8
    low_half, high_half = all_ref[:, :half], all_ref[:, half:]

    def turned(values):
        chosen = values
        for k in range(1, 4):
            chosen = jnp.where(y == k, pltpu.roll(values, half - k * shard, 1), chosen)
        return chosen

    own = turned(jnp.where(high == 0, low_half, high_half))
    other = turned(jnp.where(high == 0, high_half, low_half))
    seq = lax.axis_index("seq")
    up = lax.rem(high + seq // 16 + lax.rem(seq // 2, 8), 2) == 0
    part = shard // 2
    at = 0
    pairs = []
    for source in (own, other):
        one, three = source[:, shard : 2 * shard], source[:, 3 * shard :]
        pairs.append((jnp.where(up, one, three), jnp.where(up, three, one)))
    near, cross = pairs
    groups = [
        (own[:, :part], own[:, part:shard], near[0][:, :part], near[1][:, part:]),
        (other[:, :part], other[:, part:shard], near[1][:, :part], near[0][:, part:]),
        (own[:, 2 * shard : 2 * shard + part], own[:, 2 * shard + part : 3 * shard], cross[0][:, :part], cross[1][:, part:]),
        (other[:, 2 * shard : 2 * shard + part], other[:, 2 * shard + part : 3 * shard], cross[1][:, :part], cross[0][:, part:]),
    ]
    for group in groups:
        for low, high in (group[:2], group[2:]):
            picked_ref[:, at : at + part] = jnp.where(core == 0, low, high)
            picked_ref[:, at + part : at + 2 * part] = jnp.where(core == 0, high, low)
            at += 2 * part


def norm_kernel(halo_ref, x_ref, gain_ref, out_ref, pair_ref):
    rows, width = x_ref.shape
    gain = gain_ref[...].reshape(1, width)

    def normed(values, side):
        values = values.astype(jnp.float32)
        centred = values - jnp.mean(values, axis=-1, keepdims=True)
        var = jnp.mean(centred * centred, axis=-1, keepdims=True)
        values = centred * lax.rsqrt(var + EPSILON) * gain
        for at in range(0, width, LANES):
            pair_ref[at // LANES, pl.ds(side, HALO, stride=2), :] = values[:, at : at + LANES]

    def put(row):
        for at in range(0, width, LANES):
            out_ref[pl.ds(row, 2 * HALO), at : at + LANES] = pair_ref[at // LANES].astype(jnp.bfloat16)

    normed(halo_ref[...], 0)
    normed(x_ref[rows // 2 - HALO : rows // 2, :], 1)
    put(0)

    @pl.loop(1, rows // 2 // HALO + 1)
    def _(i):
        at = pl.multiple_of(i * HALO, HALO)
        normed(x_ref[pl.ds(at - HALO, HALO), :], 0)
        normed(x_ref[pl.ds(at + rows // 2 - HALO, HALO), :], 1)
        put(pl.multiple_of(2 * at, HALO))


def group_kernel(taps, first, tiles, last, *refs):
    nx_ref, dk_ref = refs[:2]
    pieces = refs[2:6]
    refs = refs[6:]
    if first:
        before_ref, refs = refs[0], refs[1:]
    conv_ref, s1_ref, s2_ref = refs[:3]
    refs = refs[3:]
    if not last:
        after_ref, refs = refs[0], refs[1:]
    w_ref, gated_ref = refs
    rows = conv_ref.shape[0]
    size = pieces[0].shape[1]

    def gather(tile):
        for at in range(tile * LANES, (tile + 1) * LANES, UNIT):
            piece, row = divmod(at, size)
            for side in range(2):
                to = 2 * tile * LANES + side * LANES + at % LANES
                w_ref[to : to + UNIT, :] = pieces[piece][side, row : row + UNIT, :]

    def shifted(tile):
        for k in range(1, 8):
            count = gated_ref.shape[2] - 16
            gated_ref[tile % 2, k, 0:count, :] = gated_ref[tile % 2, 0, 2 * k : 2 * k + count, :]

    s1_ref[...] = jnp.zeros_like(s1_ref)
    s2_ref[...] = jnp.zeros_like(s2_ref)

    def project(tile):
        both = lax.dot_general(
            nx_ref[...],
            w_ref[tile * 2 * LANES : (tile + 1) * 2 * LANES, :],
            (((1,), (1,)), ((), ())),
            preferred_element_type=jnp.float32,
        )
        value, gate = both[:, :LANES], both[:, LANES:]
        gated = (value * jnp.tanh(gate) + value).astype(jnp.bfloat16)
        if tile == tiles - 1 and not last:
            after_ref[...] = gated
        else:
            gated_ref[tile % 2, 0] = gated
            shifted(tile)

    def convolve(tile):
        start = (tile + bool(first)) * LANES
        lanes = slice(start, start + LANES)
        taps_at = slice((first + tile) * LANES, (first + tile + 1) * LANES)
        step, chunk = 16, 8
        source = gated_ref.at[tile % 2]
        weights = [
            jnp.broadcast_to(
                dk_ref[tap : tap + 1, taps_at], (step, LANES)
            ).astype(jnp.bfloat16)
            for tap in range(taps)
        ]
        for at in range(0, rows, step):
            total = None
            for low in range(0, taps, chunk):
                terms = []
                for tap in range(low, min(taps, low + chunk)):
                    skip, shift = divmod(HALO - (taps - 1) + tap, 8)
                    begin = 16 * skip + at
                    terms.append(weights[tap] * source[shift, begin : begin + step, :])
                while len(terms) > 1:
                    left = terms[len(terms) // 2 * 2 :]
                    terms = [p + q for p, q in zip(terms[::2], terms[1::2])] + left
                part = terms[0].astype(jnp.float32)
                total = part if total is None else total + part
            conv_ref[at : at + step, lanes] = total.astype(conv_ref.dtype)
            s1_ref[at : at + step, :] += total
            s2_ref[at : at + step, :] += total * total

    if first:
        gated_ref[1, 0] = before_ref[...]
        shifted(-1)
    gather(0)
    for tile in range(tiles):
        if tile + 1 < tiles:
            gather(tile + 1)
        project(tile)
        if tile or first:
            convolve(tile - 1)
    if last:
        convolve(tiles - 1)


def mix_kernel(count, *refs):
    x_ref, picked_ref = refs[:2]
    convs, s1s, s2s = refs[2:6], refs[6:10], refs[10:14]
    pieces = refs[14 : 14 + count]
    out_ref, w_ref, act_ref, mixed_ref = refs[14 + count :]
    size = pieces[0].shape[-2]
    for i, (index, half) in enumerate(OUT_PARTS):
        w_ref[i * size : (i + 1) * size, :] = pieces[index][half]
    rows, width = x_ref.shape
    step = act_ref.shape[1]

    def activate(block):
        at = slice(block * step, (block + 1) * step)
        mean = jnp.sum(sum(ref[at, :] for ref in s1s), axis=1, keepdims=True) / width
        var = jnp.sum(sum(ref[at, :] for ref in s2s), axis=1, keepdims=True) / width - mean * mean
        scale = lax.rsqrt(var + EPSILON)
        begin = 0
        for conv_ref in convs:
            lanes = slice(begin, begin + conv_ref.shape[1])
            begin = lanes.stop
            conv = conv_ref[at, :].astype(jnp.float32)
            mid = (conv - mean) * scale * picked_ref[32:33, lanes] + picked_ref[33:34, lanes]
            act_ref[block % 2, :, lanes] = (mid * jnp.tanh(mid) + mid).astype(jnp.bfloat16)

    def finish(block):
        tile = 2 * LANES
        for k in range(0, width, tile):
            mixed = jnp.dot(act_ref[block % 2], w_ref[:, k : k + tile], preferred_element_type=jnp.float32)
            for j in range(2):
                lanes = slice(k + j * LANES, k + (j + 1) * LANES)
                mixed_ref[lanes.start // LANES] = mixed[:, j * LANES : (j + 1) * LANES]
                for side in range(2):
                    first = side * (rows // 2) + block * (step // 2)
                    here = slice(first, first + step // 2)
                    total = mixed_ref[lanes.start // LANES, pl.ds(side, step // 2, stride=2), :]
                    out_ref[here, lanes] = (x_ref[here, lanes].astype(jnp.float32) + total).astype(out_ref.dtype)

    blocks = rows // step
    activate(0)
    for block in range(blocks):
        if block + 1 < blocks:
            activate(block + 1)
        finish(block)


def params(limit_mib):
    return pltpu.CompilerParams(vmem_limit_bytes=limit_mib * 2**20)


def spread(mine, rest):
    aside = moved(mine, ASIDE)
    cross = moved(mine, CROSS)
    swapped = moved(aside, PARTNER)
    far = moved(aside, ASIDE)
    diagonal = moved(cross, ASIDE)
    opposite = moved(far, CROSS)
    turned = moved(diagonal, PARTNER)

    def both(value):
        return [value, moved(value, SIBLING)]

    return [
        [mine, rest] + both(aside),
        both(cross) + both(swapped),
        both(far) + both(diagonal),
        both(opposite) + both(turned),
    ]


def join_kernel(a_ref, b_ref, out_ref):
    out_ref[0] = a_ref[0]
    out_ref[1] = b_ref[0]


def spread_pairs(mine, rest):
    cross = moved(mine, CROSS)
    pair = pl.pallas_call(
        join_kernel, out_shape=jax.ShapeDtypeStruct((2,) + mine.shape[1:], mine.dtype), compiler_params=params(8)
    )(mine, cross)
    aside = moved(pair, ASIDE)
    swapped = moved(aside, PARTNER)
    far = moved(aside, ASIDE)
    others = [moved(value, SIBLING) for value in (cross, aside, swapped, far)]
    return [pair, rest, others[0], aside, others[1], swapped, others[2], far, others[3]]


OUT_PARTS = (
    (0, 0), (1, 0), (3, 0), (4, 0),
    (0, 1), (2, 0), (5, 0), (6, 0),
    (7, 0), (8, 0), (3, 1), (4, 1),
    (7, 1), (8, 1), (5, 1), (6, 1),
)


def body(frames_in, norm_gain, in_weight, depth_kernel, mid_gain, mid_bias, out_weight):
    rows, width = frames_in.shape
    taps = depth_kernel.shape[0]
    bf16, f32 = jnp.bfloat16, jnp.float32
    order = [(i, i + 1) for i in range(lax.axis_size("seq") * lax.axis_size("fsdp") - 1)]
    size = in_weight.shape[2] // 2
    in_half = jax.ShapeDtypeStruct((2, size, width), bf16)
    out_half = jax.ShapeDtypeStruct((1, size, width), bf16)
    in_mine, in_rest, out_mine, out_rest, picked, last = pl.pallas_call(
        prepare_kernel,
        in_specs=[pl.BlockSpec(memory_space=pltpu.HBM)] * 6,
        out_shape=(
            in_half,
            in_half,
            out_half,
            out_half,
            jax.ShapeDtypeStruct((40, width), f32),
            jax.ShapeDtypeStruct((HALO, width), bf16),
        ),
        scratch_shapes=[
            pltpu.VMEM((2, 2, size, width), f32),
            pltpu.VMEM((2, size, width), f32),
            pltpu.VMEM((40, width), f32),
            pltpu.VMEM((taps, width), f32),
            pltpu.VMEM((width,), f32),
            pltpu.VMEM((width,), f32),
            pltpu.SemaphoreType.DMA((10,)),
        ],
        compiler_params=params(16),
        name="prepare",
    )(
        *[
            pltpu.with_memory_space_constraint(value, pltpu.HBM)
            for value in (jnp.transpose(in_weight, (1, 2, 0)), out_weight, depth_kernel, mid_gain, mid_bias, frames_in)
        ]
    )
    halo = moved(last, order)
    in_pieces = spread(in_mine, in_rest)
    pieces = spread_pairs(out_mine, out_rest)

    normed = pl.pallas_call(
        norm_kernel,
        out_shape=jax.ShapeDtypeStruct((rows + 2 * HALO, width), bf16),
        scratch_shapes=[pltpu.VMEM((width // LANES, 2 * HALO, LANES), f32)],
        compiler_params=params(16),
        name="norm",
    )(halo, frames_in, norm_gain)

    tiles = width // 4 // LANES
    convs, sums, squares, carried = [], [], [], []
    for index, parts in enumerate(in_pieces):
        last = index == len(in_pieces) - 1
        first = index * tiles
        done = (tiles + last - (not first)) * LANES
        shapes = [
            jax.ShapeDtypeStruct((rows, done), bf16),
            jax.ShapeDtypeStruct((rows, LANES), f32),
            jax.ShapeDtypeStruct((rows, LANES), f32),
        ]
        if not last:
            shapes.append(jax.ShapeDtypeStruct((rows + 2 * HALO, LANES), bf16))
        conv, total, square, *carry = pl.pallas_call(
            functools.partial(group_kernel, taps, first, tiles, last),
            out_shape=tuple(shapes),
            scratch_shapes=[
                pltpu.VMEM((2 * tiles * LANES, width), bf16),
                pltpu.VMEM((2, 8, rows + 2 * HALO, LANES), bf16),
            ],
            compiler_params=params(16),
            cost_estimate=pl.CostEstimate(
                flops=4 * rows * width * tiles * LANES, bytes_accessed=2**22, transcendentals=rows * tiles * LANES
            ),
        )(normed, picked, *parts, *carried)
        convs.append(conv)
        sums.append(total)
        squares.append(square)
        carried = carry
    return pl.pallas_call(
        lambda *refs: mix_kernel(len(pieces), *refs),
        out_shape=jax.ShapeDtypeStruct((rows, width), bf16),
        scratch_shapes=[
            pltpu.VMEM((width, width), bf16),
            pltpu.VMEM((2, 256, width), bf16),
            pltpu.VMEM((width // LANES, 256, LANES), f32),
        ],
        compiler_params=params(24),
        cost_estimate=pl.CostEstimate(
            flops=2 * rows * width * width, bytes_accessed=width * width * 2, transcendentals=rows * width
        ),
        name="mix",
    )(frames_in, picked, *convs, *sums, *squares, *pieces)


def solution(mesh):
    placed = (P(AXES, None), P(), P(None, None, "fsdp"), P(), P(), P(), P("fsdp", None))

    return jax.shard_map(body, mesh=mesh, in_specs=placed, out_specs=P(AXES, None), check_vma=False)
```

```python
import functools

import jax
import jax.numpy as jnp
from jax import lax
from jax.experimental import pallas as pl
from jax.experimental.pallas import tpu as pltpu
from jax.sharding import PartitionSpec as P

EPSILON = 1e-05
AXES = ("seq", "fsdp")
HALO = 32
LANES = 128


def place(x, y, z, core):
    x, y, z, core = x % 4, y % 4, z % 8, core % 2
    return (((x % 2) * 8 + z) * 2 + core) * 8 + (x // 2) * 4 + y


def route(target):
    return [
        (place(x, y, z, c), place(*target(x, y, z, c)))
        for x in range(4)
        for y in range(4)
        for z in range(8)
        for c in range(2)
    ]


def colour(x, z):
    return ((x // 2) ^ x ^ z) & 1


ASIDE = route(lambda x, y, z, c: (x, y - 1 if c == colour(x, z) else y + 1, z, c))
PARTNER = route(lambda x, y, z, c: (x ^ 1, y, z, c) if c == 0 else (x, y, z ^ 1, c))
CROSS = route(lambda x, y, z, c: (((x + 1) ^ 1) - 1, y, z, c))
SIBLING = route(lambda x, y, z, c: (x, y, z, 1 - c))
UNIT = 32


def moved(value, pairs):
    return lax.ppermute(value, AXES, pairs)


def my_core():
    return lax.rem(lax.axis_index("seq"), 2)


def prepare_kernel(w_in, w_out, taps_in, gain_in, bias_in, frames_in, *refs):
    in_mine, in_rest, out_mine, out_rest, picked_ref, halo_ref, in_v, out_v, all_ref, taps_v, gain_v, bias_v, sems = refs
    core = my_core()
    size = in_mine.shape[1]
    taps, width = taps_in.shape
    halves = [pl.ds(pl.multiple_of(which * size, UNIT), size) for which in (core, 1 - core)]
    pairs = [(w_in.at[side, part], in_v.at[side, k]) for side in range(2) for k, part in enumerate(halves)]
    pairs += [(w_out.at[part], out_v.at[k]) for k, part in enumerate(halves)]
    pairs += [
        (taps_in, taps_v),
        (gain_in, gain_v),
        (bias_in, bias_v),
        (frames_in.at[frames_in.shape[0] - HALO :], halo_ref),
    ]
    copies = [pltpu.make_async_copy(source, target, sems.at[i]) for i, (source, target) in enumerate(pairs)]
    for copy in copies:
        copy.start()
    for side in range(2):
        for k, out_ref in enumerate((in_mine, in_rest)):
            copies[2 * side + k].wait()
            out_ref[side] = (0.5 * in_v[side, k]).astype(jnp.bfloat16)
    for k, out_ref in enumerate((out_mine, out_rest)):
        copies[4 + k].wait()
        out_ref[0] = out_v[k].astype(jnp.bfloat16)
    for copy in copies[6:]:
        copy.wait()
    all_ref[0:taps, :] = taps_v[...]
    all_ref[32:33, :] = 0.5 * gain_v[...].reshape(1, width)
    all_ref[33:34, :] = 0.5 * bias_v[...].reshape(1, width)
    at = lax.axis_index("fsdp")
    high, y = at // 4, lax.rem(at, 4)
    half, shard = width // 2, width // 8
    low_half, high_half = all_ref[:, :half], all_ref[:, half:]

    def turned(values):
        chosen = values
        for k in range(1, 4):
            chosen = jnp.where(y == k, pltpu.roll(values, half - k * shard, 1), chosen)
        return chosen

    own = turned(jnp.where(high == 0, low_half, high_half))
    other = turned(jnp.where(high == 0, high_half, low_half))
    seq = lax.axis_index("seq")
    up = lax.rem(high + seq // 16 + lax.rem(seq // 2, 8), 2) == 0
    part = shard // 2
    at = 0
    pairs = []
    for source in (own, other):
        one, three = source[:, shard : 2 * shard], source[:, 3 * shard :]
        pairs.append((jnp.where(up, one, three), jnp.where(up, three, one)))
    near, cross = pairs
    groups = [
        (own[:, :part], own[:, part:shard], near[0][:, :part], near[1][:, part:]),
        (other[:, :part], other[:, part:shard], near[1][:, :part], near[0][:, part:]),
        (own[:, 2 * shard : 2 * shard + part], own[:, 2 * shard + part : 3 * shard], cross[0][:, :part], cross[1][:, part:]),
        (other[:, 2 * shard : 2 * shard + part], other[:, 2 * shard + part : 3 * shard], cross[1][:, :part], cross[0][:, part:]),
    ]
    for group in groups:
        for low, high in (group[:2], group[2:]):
            picked_ref[:, at : at + part] = jnp.where(core == 0, low, high)
            picked_ref[:, at + part : at + 2 * part] = jnp.where(core == 0, high, low)
            at += 2 * part


def normed_pairs(first, second, gain, pair_ref, out_ref, row):
    width = out_ref.shape[1]
    for side, values in enumerate((first, second)):
        values = values.astype(jnp.float32)
        centred = values - jnp.mean(values, axis=-1, keepdims=True)
        var = jnp.mean(centred * centred, axis=-1, keepdims=True)
        values = centred * lax.rsqrt(var + EPSILON) * gain
        for at in range(0, width, LANES):
            pair_ref[at // LANES, pl.ds(side, HALO, stride=2), :] = values[:, at : at + LANES]
    for at in range(0, width, LANES):
        out_ref[pl.ds(row, 2 * HALO), at : at + LANES] = pair_ref[at // LANES].astype(jnp.bfloat16)


def norm_kernel(x_ref, gain_ref, out_ref, pair_ref):
    rows, width = x_ref.shape
    gain = gain_ref[...].reshape(1, width)

    @pl.loop(0, rows // 2 // HALO)
    def _(i):
        at = pl.multiple_of(i * HALO, HALO)
        later = pl.multiple_of(at + rows // 2, HALO)
        normed_pairs(
            x_ref[pl.ds(at, HALO), :],
            x_ref[pl.ds(later, HALO), :],
            gain,
            pair_ref,
            out_ref,
            pl.multiple_of(2 * at, HALO),
        )


def head_kernel(halo_ref, x_ref, gain_ref, out_ref, pair_ref):
    rows, width = x_ref.shape
    gain = gain_ref[...].reshape(1, width)
    normed_pairs(halo_ref[...], x_ref[rows // 2 - HALO : rows // 2, :], gain, pair_ref, out_ref, 0)


def group_kernel(taps, first, tiles, last, *refs):
    head_ref, nx_ref, dk_ref = refs[:3]
    pieces = refs[3:7]
    refs = refs[7:]
    if first:
        before_ref, refs = refs[0], refs[1:]
    conv_ref, s1_ref, s2_ref = refs[:3]
    refs = refs[3:]
    if not last:
        after_ref, refs = refs[0], refs[1:]
    w_ref, gated_ref = refs
    rows = conv_ref.shape[0]
    size = pieces[0].shape[1]

    def gather(tile):
        for at in range(tile * LANES, (tile + 1) * LANES, UNIT):
            piece, row = divmod(at, size)
            for side in range(2):
                to = 2 * tile * LANES + side * LANES + at % LANES
                w_ref[to : to + UNIT, :] = pieces[piece][side, row : row + UNIT, :]

    def shifted(tile):
        for k in range(1, 8):
            count = gated_ref.shape[2] - 16
            gated_ref[tile % 2, k, 0:count, :] = gated_ref[tile % 2, 0, 2 * k : 2 * k + count, :]

    s1_ref[...] = jnp.zeros_like(s1_ref)
    s2_ref[...] = jnp.zeros_like(s2_ref)

    def project(tile):
        both = lax.dot_general(
            jnp.concatenate([head_ref[...], nx_ref[...]], axis=0),
            w_ref[tile * 2 * LANES : (tile + 1) * 2 * LANES, :],
            (((1,), (1,)), ((), ())),
            preferred_element_type=jnp.float32,
        )
        value, gate = both[:, :LANES], both[:, LANES:]
        gated = (value * jnp.tanh(gate) + value).astype(jnp.bfloat16)
        if tile == tiles - 1 and not last:
            after_ref[...] = gated
        else:
            gated_ref[tile % 2, 0] = gated
            shifted(tile)

    def convolve(tile):
        start = (tile + bool(first)) * LANES
        lanes = slice(start, start + LANES)
        taps_at = slice((first + tile) * LANES, (first + tile + 1) * LANES)
        step = 16
        source = gated_ref.at[tile % 2]
        weights = [
            jnp.broadcast_to(dk_ref[tap : tap + 1, taps_at], (step, LANES)).astype(jnp.bfloat16) for tap in range(taps)
        ]
        for at in range(0, rows, step):
            terms = []
            for tap in range(taps):
                skip, shift = divmod(HALO - (taps - 1) + tap, 8)
                begin = 16 * skip + at
                term, level = weights[tap] * source[shift, begin : begin + step, :], 0
                while terms and terms[-1][1] == level:
                    term, level = terms.pop()[0] + term, level + 1
                terms.append((term, level))
            while len(terms) > 1:
                right, left = terms.pop(), terms.pop()
                terms.append((left[0] + right[0], 0))
            terms = [terms[0][0]]
            conv_ref[at : at + step, lanes] = terms[0]
            total = terms[0].astype(jnp.float32)
            s1_ref[at : at + step, :] += total
            s2_ref[at : at + step, :] += total * total

    if first:
        gated_ref[1, 0] = before_ref[...]
        shifted(-1)
    gather(0)
    for tile in range(tiles):
        if tile + 1 < tiles:
            gather(tile + 1)
        project(tile)
        if tile or first:
            convolve(tile - 1)
    if last:
        convolve(tiles - 1)


def mix_kernel(count, *refs):
    x_ref, picked_ref = refs[:2]
    convs, s1s, s2s = refs[2:6], refs[6:10], refs[10:14]
    pieces = refs[14 : 14 + count]
    out_ref, w_ref, act_ref, mixed_ref = refs[14 + count :]
    size = pieces[0].shape[-2]
    for i, (index, half) in enumerate(OUT_PARTS):
        w_ref[i * size : (i + 1) * size, :] = pieces[index][half]
    rows, width = x_ref.shape
    step = act_ref.shape[1]

    def activate(block):
        at = slice(block * step, (block + 1) * step)
        mean = jnp.sum(sum(ref[at, :] for ref in s1s), axis=1, keepdims=True) / width
        var = jnp.sum(sum(ref[at, :] for ref in s2s), axis=1, keepdims=True) / width - mean * mean
        scale = lax.rsqrt(var + EPSILON)
        begin = 0
        for conv_ref in convs:
            lanes = slice(begin, begin + conv_ref.shape[1])
            begin = lanes.stop
            conv = conv_ref[at, :].astype(jnp.float32)
            mid = (conv - mean) * scale * picked_ref[32:33, lanes] + picked_ref[33:34, lanes]
            act_ref[block % 2, :, lanes] = (mid * jnp.tanh(mid) + mid).astype(jnp.bfloat16)

    def finish(block):
        tile = 2 * LANES
        for k in range(0, width, tile):
            mixed = jnp.dot(act_ref[block % 2], w_ref[:, k : k + tile], preferred_element_type=jnp.float32)
            for j in range(2):
                lanes = slice(k + j * LANES, k + (j + 1) * LANES)
                mixed_ref[lanes.start // LANES] = mixed[:, j * LANES : (j + 1) * LANES]
                for side in range(2):
                    first = side * (rows // 2) + block * (step // 2)
                    here = slice(first, first + step // 2)
                    total = mixed_ref[lanes.start // LANES, pl.ds(side, step // 2, stride=2), :]
                    out_ref[here, lanes] = (x_ref[here, lanes].astype(jnp.float32) + total).astype(out_ref.dtype)

    blocks = rows // step
    activate(0)
    for block in range(blocks):
        if block + 1 < blocks:
            activate(block + 1)
        finish(block)


def params(limit_mib):
    return pltpu.CompilerParams(vmem_limit_bytes=limit_mib * 2**20)


def spread(mine, rest):
    aside = moved(mine, ASIDE)
    cross = moved(mine, CROSS)
    swapped = moved(aside, PARTNER)
    far = moved(aside, ASIDE)
    diagonal = moved(cross, ASIDE)
    opposite = moved(far, CROSS)
    turned = moved(diagonal, PARTNER)

    def both(value):
        return [value, moved(value, SIBLING)]

    return [
        [mine, rest] + both(aside),
        both(cross) + both(swapped),
        both(far) + both(diagonal),
        both(opposite) + both(turned),
    ]


def join_kernel(a_ref, b_ref, out_ref):
    out_ref[0] = a_ref[0]
    out_ref[1] = b_ref[0]


def spread_pairs(mine, rest):
    cross = moved(mine, CROSS)
    pair = pl.pallas_call(
        join_kernel, out_shape=jax.ShapeDtypeStruct((2,) + mine.shape[1:], mine.dtype), compiler_params=params(8)
    )(mine, cross)
    aside = moved(pair, ASIDE)
    swapped = moved(aside, PARTNER)
    far = moved(aside, ASIDE)
    others = [moved(value, SIBLING) for value in (cross, aside, swapped, far)]
    return [pair, rest, others[0], aside, others[1], swapped, others[2], far, others[3]]


OUT_PARTS = (
    (0, 0), (1, 0), (3, 0), (4, 0),
    (0, 1), (2, 0), (5, 0), (6, 0),
    (7, 0), (8, 0), (3, 1), (4, 1),
    (7, 1), (8, 1), (5, 1), (6, 1),
)


def body(frames_in, norm_gain, in_weight, depth_kernel, mid_gain, mid_bias, out_weight):
    rows, width = frames_in.shape
    taps = depth_kernel.shape[0]
    bf16, f32 = jnp.bfloat16, jnp.float32
    order = [(i, i + 1) for i in range(lax.axis_size("seq") * lax.axis_size("fsdp") - 1)]
    size = in_weight.shape[2] // 2
    in_half = jax.ShapeDtypeStruct((2, size, width), bf16)
    out_half = jax.ShapeDtypeStruct((1, size, width), bf16)
    in_mine, in_rest, out_mine, out_rest, picked, last = pl.pallas_call(
        prepare_kernel,
        in_specs=[pl.BlockSpec(memory_space=pltpu.HBM)] * 6,
        out_shape=(
            in_half,
            in_half,
            out_half,
            out_half,
            jax.ShapeDtypeStruct((40, width), f32),
            jax.ShapeDtypeStruct((HALO, width), bf16),
        ),
        scratch_shapes=[
            pltpu.VMEM((2, 2, size, width), f32),
            pltpu.VMEM((2, size, width), f32),
            pltpu.VMEM((40, width), f32),
            pltpu.VMEM((taps, width), f32),
            pltpu.VMEM((width,), f32),
            pltpu.VMEM((width,), f32),
            pltpu.SemaphoreType.DMA((10,)),
        ],
        compiler_params=params(16),
        name="prepare",
    )(
        *[
            pltpu.with_memory_space_constraint(value, pltpu.HBM)
            for value in (jnp.transpose(in_weight, (1, 2, 0)), out_weight, depth_kernel, mid_gain, mid_bias, frames_in)
        ]
    )
    halo = moved(last, order)
    in_pieces = spread(in_mine, in_rest)
    pieces = spread_pairs(out_mine, out_rest)

    pair = pltpu.VMEM((width // LANES, 2 * HALO, LANES), f32)
    normed = pl.pallas_call(
        norm_kernel,
        out_shape=jax.ShapeDtypeStruct((rows, width), bf16),
        scratch_shapes=[pair],
        compiler_params=params(16),
        name="norm",
    )(frames_in, norm_gain)
    head = pl.pallas_call(
        head_kernel,
        out_shape=jax.ShapeDtypeStruct((2 * HALO, width), bf16),
        scratch_shapes=[pair],
        compiler_params=params(16),
        name="head",
    )(halo, frames_in, norm_gain)
    tiles = width // 4 // LANES
    convs, sums, squares, carried = [], [], [], []
    for index, parts in enumerate(in_pieces):
        last = index == len(in_pieces) - 1
        first = index * tiles
        done = (tiles + last - (not first)) * LANES
        shapes = [
            jax.ShapeDtypeStruct((rows, done), bf16),
            jax.ShapeDtypeStruct((rows, LANES), f32),
            jax.ShapeDtypeStruct((rows, LANES), f32),
        ]
        if not last:
            shapes.append(jax.ShapeDtypeStruct((rows + 2 * HALO, LANES), bf16))
        conv, total, square, *carry = pl.pallas_call(
            functools.partial(group_kernel, taps, first, tiles, last),
            out_shape=tuple(shapes),
            scratch_shapes=[
                pltpu.VMEM((2 * tiles * LANES, width), bf16),
                pltpu.VMEM((2, 8, rows + 2 * HALO, LANES), bf16),
            ],
            compiler_params=params(16),
            cost_estimate=pl.CostEstimate(
                flops=4 * rows * width * tiles * LANES, bytes_accessed=2**22, transcendentals=rows * tiles * LANES
            ),
        )(head, normed, picked, *parts, *carried)
        convs.append(conv)
        sums.append(total)
        squares.append(square)
        carried = carry
    return pl.pallas_call(
        lambda *refs: mix_kernel(len(pieces), *refs),
        out_shape=jax.ShapeDtypeStruct((rows, width), bf16),
        scratch_shapes=[
            pltpu.VMEM((width, width), bf16),
            pltpu.VMEM((2, 256, width), bf16),
            pltpu.VMEM((width // LANES, 256, LANES), f32),
        ],
        compiler_params=params(24),
        cost_estimate=pl.CostEstimate(
            flops=2 * rows * width * width, bytes_accessed=width * width * 2, transcendentals=rows * width
        ),
        name="mix",
    )(frames_in, picked, *convs, *sums, *squares, *pieces)


def solution(mesh):
    placed = (P(AXES, None), P(), P(None, None, "fsdp"), P(), P(), P(), P("fsdp", None))

    return jax.shard_map(body, mesh=mesh, in_specs=placed, out_specs=P(AXES, None), check_vma=False)
```
